256 devices in a mesh: row: 8 (over x, core), cls: 32 (over y, z).
Axes of the slice: x: 4, y: 4, z: 8, core: 2. Of those that a mesh axis runs over, the one named last changes fastest.
Arguments:
- images: bfloat16 [16384, 512], P('row'), may hold values from -6 to 6
- image_index: int32 [8192], P('row'), may hold values from 0 to 16383, as said below
- labels: int32 [8192], P('row'), may hold values from 0 to 21503
- counts: int32 [8192], P('row'), may hold values from 1 to 10
- projection: bfloat16 [2, 512, 512], P(None, None, 'cls'), may hold values from -0.25 to 0.25
- phase_shift: bfloat16 [2, 512], P(None, 'cls'), may hold values from 0 to 6.28125
- predictions: bfloat16 [8192, 21504], P('row', 'cls'), may hold values from -20 to 20
- block_weights: bfloat16 [2, 512, 21504], P(None, None, 'cls'), may hold values from -3 to 3
Outputs:
- updated_weights: float32 [2, 512, 21504], P(None, None, 'cls')
- residual_tiles: float32 [8192, 21504], P('row', 'cls')
- weighted_loss: float32 [], replicated
The draws below stay inside these ranges and needn't reach their ends.
Inputs may be any that keep to these rules, and one draw needn't show every extreme that they name: `image_index`: row r names one of the 2048 images that begin at (r // 1024) * 2048.
All inputs are finite; a program needn't handle non-finite values.
Results may differ from the reference program's by a relative error of at most 0.0086.
Values may be sent and summed in bfloat16 or wider, within the bound.
No kernel may reach another device: no remote copies, remote signals or barrier semaphores. Data moves between devices by JAX's collectives and lax.ppermute only.
A program may use at most 128 MiB of HBM per device.

```python
import math
import jax
import jax.numpy as jnp
import numpy as np

DIN = 512
BLK = 512
K = 21504
NBLK = 2
ROW_DEV = 1024
POOL_DEV = 2048
ROWS = 8192
POOL = 16384


def pinned(key, values, low_value, high_value):
    blocks = ROWS // ROW_DEV
    positions = jnp.arange(ROWS, dtype=jnp.int32)
    block_of = positions // ROW_DEV
    within = positions % ROW_DEV
    key_high, key_gap = jax.random.split(key)
    high_pos = jax.random.randint(key_high, (blocks,), 0, ROW_DEV).astype(jnp.int32)
    low_pos = (high_pos + 1 + jax.random.randint(key_gap, (blocks,), 0, ROW_DEV - 1).astype(jnp.int32)) % ROW_DEV
    values = jnp.where(within == high_pos[block_of], high_value, values)
    return jnp.where(within == low_pos[block_of], low_value, values)


def draw_image_index(key, part):
    key_inside, key_pin = jax.random.split(jax.random.fold_in(key, 11))
    inside = jax.random.randint(key_inside, (ROWS,), 0, POOL_DEV).astype(jnp.int32)
    inside = pinned(key_pin, inside, 0, POOL_DEV - 1)
    block_of = jnp.arange(ROWS, dtype=jnp.int32) // ROW_DEV
    return (block_of * POOL_DEV + inside).astype(jnp.int32)


def draw_counts(key, part):
    key_draw, key_pin = jax.random.split(jax.random.fold_in(key, 23))
    blocks = ROWS // ROW_DEV
    block_of = jnp.arange(ROWS, dtype=jnp.int32) // ROW_DEV
    upper = 3 + 8 * block_of // max(blocks - 1, 1)
    drawn = jax.random.randint(key_draw, (ROWS,), 1, upper).astype(jnp.int32)
    return pinned(key_pin, drawn, 1, upper - 1).astype(jnp.int32)


def draw_predictions(key, part):
    key_base, key_row = jax.random.split(jax.random.fold_in(key, 37))
    column = jnp.arange(K, dtype=jnp.float32)
    col_scale = 0.1 * jnp.power(10.0, column / max(K - 1, 1))
    row_scale = jnp.exp(jax.random.uniform(key_row, (ROWS, 1), jnp.float32, -1.15, 1.15))
    base = jax.random.normal(key_base, (ROWS, K), jnp.float32)
    return jnp.clip(base * col_scale[None, :] * row_scale, -20.0, 20.0).astype(jnp.bfloat16)


def set_ends(values, key, least, top_value):
    longest = values.shape.index(max(values.shape))
    spots = []
    for shift in (0, 1):
        where = [jax.random.randint(jax.random.fold_in(key, axis), (), 0, length) for axis, length in enumerate(values.shape)]
        where[longest] = (where[longest] + shift) % values.shape[longest]
        spots.append(tuple(where))
    return values.at[spots[0]].set(least).at[spots[1]].set(top_value)


def steps_of(rng, dims, shards, low, high):
    factor_of, own = 1.0, jax.random.fold_in(rng, 6)
    for axis_at, blocks in shards:
        heights = jnp.exp(jax.random.uniform(jax.random.fold_in(own, axis_at), (blocks,), jnp.float32, low / len(shards), high / len(shards)))
        factor_of = factor_of * jnp.repeat(heights, dims[axis_at] // blocks).reshape([-1 if axis == axis_at else 1 for axis in range(len(dims))])
    return factor_of


def rank_table(number_of, lean):
    loads = [(1 << 20) // math.isqrt(rank ** lean) + 1 for rank in range(1, number_of + 1)]
    width = 1 + sum(loads) // (1 << 30)
    return np.cumsum(np.array([max(1, weight // width) for weight in loads]))


def ranked(key, shape, count, skew):
    grid = rank_table(count, skew)
    lot = jax.random.randint(jax.random.fold_in(key, 1), shape, 0, int(grid[count - 1]))
    rank = jnp.searchsorted(jnp.asarray(grid, jnp.int32), lot, side="right")
    return jax.random.permutation(jax.random.fold_in(key, 2), count)[rank].astype(jnp.int32)


def gaussian(rng, extent, width, limit, pieces=(), kind=jnp.bfloat16):
    array = jax.random.normal(rng, extent, jnp.float32) * width
    if len(pieces) > 0:
        array = steps_of(rng, extent, pieces, -0.22, 0.18) * array
    return jnp.clip(array, min=-limit, max=limit).astype(kind)


def setup_inputs(seed: int = 0) -> dict:
    seeds = jax.random.split(jax.random.key(seed), 9)
    images = gaussian(seeds[0], (POOL, DIN), 1.0, 6.0, ((0, 8),))
    image_index = draw_image_index(jax.random.fold_in(seeds[8], 71), 0)
    labels = set_ends(ranked(seeds[2], (ROWS,), K, 2), jax.random.fold_in(seeds[2], 3), 0, K - 1).astype(jnp.int32)
    counts = draw_counts(jax.random.fold_in(seeds[8], 71), 0)
    projection = gaussian(seeds[4], (NBLK, DIN, BLK), DIN ** -0.5, 0.25, ((2, 32),))
    phase_shift = jnp.clip(6.28125 * jax.random.uniform(seeds[5], (NBLK, BLK), jnp.float32) ** steps_of(seeds[5], (NBLK, BLK), ((1, 32),), -0.2, 0.2), 0.0, 6.28125).astype(jnp.bfloat16)
    predictions = draw_predictions(jax.random.fold_in(seeds[8], 71), 0)
    block_weights = gaussian(seeds[7], (NBLK, BLK, K), 0.5, 3.0, ((2, 32),))
    return {"images": images, "image_index": image_index, "labels": labels, "counts": counts, "projection": projection, "phase_shift": phase_shift, "predictions": predictions, "block_weights": block_weights}


amplitude = 1.4142135623730951
penalty = 0.1

def make_features(picked, weights, offsets):
    mixed = jnp.dot(picked.astype(jnp.float32), weights.astype(jnp.float32), preferred_element_type=jnp.float32)
    return (amplitude * jnp.cos(mixed + offsets.astype(jnp.float32)[None, :])).astype(jnp.bfloat16)

def solve_block(matrix, right_side):
    factor = jnp.linalg.cholesky(matrix)
    return jax.scipy.linalg.cho_solve((factor, True), right_side)

def reference(images, image_index, labels, counts, projection, phase_shift, predictions, block_weights):
    picked = images[image_index]
    row_weights = counts.astype(jnp.float32)
    count_sum = jnp.sum(row_weights)
    classes = jnp.arange(K, dtype=jnp.int32)
    residual = (labels[:, None] == classes[None, :]).astype(jnp.float32) - predictions.astype(jnp.float32)
    identity = jnp.eye(BLK, dtype=jnp.float32)
    updated = []
    for block in range(NBLK):
        features = make_features(picked, projection[block], phase_shift[block])
        weighted = (row_weights[:, None] * features.astype(jnp.float32)).astype(jnp.bfloat16)
        normal_matrix = jnp.dot(weighted.T.astype(jnp.float32), features.astype(jnp.float32), preferred_element_type=jnp.float32) / count_sum + penalty * identity
        rounded_residual = residual.astype(jnp.bfloat16)
        right_side = jnp.dot(weighted.T.astype(jnp.float32), rounded_residual.astype(jnp.float32), preferred_element_type=jnp.float32) / count_sum - penalty * block_weights[block].astype(jnp.float32)
        change = solve_block(normal_matrix, right_side)
        updated.append(block_weights[block].astype(jnp.float32) + change)
        residual = residual - jnp.dot(features.astype(jnp.float32), change.astype(jnp.bfloat16).astype(jnp.float32), preferred_element_type=jnp.float32)
    row_share = row_weights / count_sum
    weighted_loss = jnp.sum(row_share[:, None] * residual * residual) / K
    return (jnp.stack(updated), residual, weighted_loss)
```

```python
import functools

import jax
import jax.numpy as jnp
from jax import lax
from jax.experimental import pallas as pl
from jax.experimental.pallas import tpu as pltpu
from jax.sharding import Mesh
from jax.sharding import PartitionSpec as P

CLS = ("cls_0", "cls_1")
ROW = ("row_0", "row_1")
X, CORE = ROW
Y, Z = CLS

AMPLITUDE = 1.4142135623730951
PENALTY = 0.1
HALF_COS = (
    1.0,
    -0.125,
    0.0026041666666666665,
    -2.170138888888889e-05,
    9.68812003968254e-08,
    -2.6911444554673722e-10,
    5.096864498609e-13,
)
INV_TWO_PI = 0.15915494309189535
TWO_PI_HIGH = 6.28125
TWO_PI_LOW = 0.0019353071795864769
NT = (((1,), (1,)), ((), ()))
NN = (((1,), (0,)), ((), ()))
FAST_NORM = 12.0
VMEM = pltpu.CompilerParams(vmem_limit_bytes=56 << 20)


def dot(a, b, dims=NN, precision=None):
    return lax.dot_general(a, b, dims, precision=precision, preferred_element_type=jnp.float32)


def split(x):
    high = x.astype(jnp.bfloat16)
    low = (x - high.astype(jnp.float32)).astype(jnp.bfloat16)
    return high, low


def dot3(ah, al, bh, bl):
    return dot(ah, bh) + (dot(ah, bl) + dot(al, bh))


def scaled_cos(x):
    turns = jnp.floor(x * INV_TWO_PI + 0.5)
    r = (x - turns * TWO_PI_HIGH) - turns * TWO_PI_LOW
    z = r * r
    c = jnp.full_like(z, HALF_COS[6])
    for k in range(5, -1, -1):
        c = c * z + HALF_COS[k]
    return (2.0 * AMPLITUDE) * (c * c) - AMPLITUDE


def partner(array, axes, offset):
    count = lax.axis_size(axes)
    return lax.ppermute(array, axes, [(i, i ^ offset) for i in range(count)])


def from_others(array, axes):
    return [partner(array, axes, offset) for offset in range(1, lax.axis_size(axes))]


def summed(array, axes):
    return functools.reduce(jnp.add, from_others(array, axes), array)


def gathered(array, axes):
    return jnp.stack([array] + from_others(array, axes))


def features_kernel(
    place_ref, own_ref, other_ref, picked_ref, counts_ref, feat_ref, weighted_ref, mine_ref, theirs_ref, proj_ref
):
    step = pl.program_id(0)
    slot, core = place_ref[0], place_ref[1]
    fs, din = own_ref.shape[1], picked_ref.shape[1]
    rows = proj_ref.shape[0]
    per = rows // fs
    inner = own_ref.shape[0] // per
    block, group = step // inner, step % inner
    for k in range(per):
        at = (group * per + k) ^ slot
        proj_ref[k * fs : (k + 1) * fs, :] = jnp.where(
            block == core, own_ref[at].astype(jnp.float32), other_ref[at].astype(jnp.float32)
        ).astype(jnp.bfloat16)
    mixed = dot(proj_ref[:, 0:din], picked_ref[...], NT)
    feats = scaled_cos(mixed + proj_ref[:, din : din + 1].astype(jnp.float32)).astype(jnp.bfloat16)
    at = pl.ds(pl.multiple_of(step * rows, rows), rows)
    feat_ref[at, :] = feats
    weighted_ref[at, :] = (feats.astype(jnp.float32) * counts_ref[...]).astype(jnp.bfloat16)

    @pl.when(step == pl.num_programs(0) - 1)
    def _():
        half = feat_ref.shape[0] // 2
        part = fs // 2
        first = pl.multiple_of(slot * fs, fs)
        lead = feat_ref[pl.ds(first, fs), :]
        later = feat_ref[pl.ds(pl.multiple_of(half + first, fs), fs), :]
        both = dot(jnp.concatenate([lead, later], axis=0), weighted_ref[...], NT)
        parts = (both[0:fs, 0:half], both[fs:, half:], both[0:fs, half:])
        for k, value in enumerate(parts):
            mine_ref[k] = jnp.where(core == 0, value[0:part], value[part:])
            theirs_ref[k] = jnp.where(core == 0, value[part:], value[0:part])


def make_features(place, own, other, picked, counts_row):
    cls, fs, wide = own.shape
    rows, din = picked.shape
    total = 2 * cls * fs
    per = max(1, 128 // fs)
    whole = pl.BlockSpec((cls, fs, wide), lambda i: (0, 0, 0))
    part = pl.BlockSpec((3, fs // 2, total // 2), lambda i: (0, 0, 0))
    feature = pl.BlockSpec((total, rows), lambda i: (0, 0))
    return pl.pallas_call(
        features_kernel,
        grid=(2 * cls // per,),
        in_specs=[
            pl.BlockSpec(memory_space=pltpu.SMEM),
            whole,
            whole,
            pl.BlockSpec((rows, din), lambda i: (0, 0)),
            pl.BlockSpec((1, rows), lambda i: (0, 0)),
        ],
        out_specs=[feature, feature, part, part],
        out_shape=[
            jax.ShapeDtypeStruct((total, rows), jnp.bfloat16),
            jax.ShapeDtypeStruct((total, rows), jnp.bfloat16),
            jax.ShapeDtypeStruct((3, fs // 2, total // 2), jnp.float32),
            jax.ShapeDtypeStruct((3, fs // 2, total // 2), jnp.float32),
        ],
        scratch_shapes=[pltpu.VMEM((per * fs, wide), jnp.bfloat16)],
        compiler_params=VMEM,
        name="features",
    )(place, own, other, picked, counts_row)


def start_residual(start, labels, preds):
    classes = start + lax.broadcasted_iota(jnp.int32, preds.shape, 0)
    return jnp.where(labels == classes, 1.0, 0.0) - preds.astype(jnp.float32)


def corr_kernel(place_ref, weighted_ref, labels_ref, preds_ref, mine_ref, theirs_ref):
    tile = preds_ref.shape[0]
    lanes = mine_ref.shape[2]
    slot, core, x = place_ref[0], place_ref[1], place_ref[2]
    start = slot * (tile * pl.num_programs(0)) + pl.program_id(0) * tile
    residual = start_residual(start, labels_ref[...], preds_ref[...])
    sums = dot(residual.astype(jnp.bfloat16), weighted_ref[...], NT)
    for k in range(mine_ref.shape[0]):
        even = sums[:, 2 * k * lanes : (2 * k + 1) * lanes]
        odd = sums[:, (2 * k + 1) * lanes : (2 * k + 2) * lanes]
        mine_ref[k ^ x] = jnp.where(core == 0, even, odd)
        theirs_ref[k ^ x] = jnp.where(core == 0, odd, even)


def make_corr(place, weighted, labels_row, preds, tiles):
    width, rows = preds.shape
    total = weighted.shape[0]
    tile = width // tiles
    half = jax.ShapeDtypeStruct((4, width, total // 8), jnp.float32)
    half_spec = pl.BlockSpec((4, tile, total // 8), lambda i: (0, i, 0))
    return pl.pallas_call(
        corr_kernel,
        grid=(tiles,),
        in_specs=[
            pl.BlockSpec(memory_space=pltpu.SMEM),
            pl.BlockSpec((total, rows), lambda i: (0, 0)),
            pl.BlockSpec((1, rows), lambda i: (0, 0)),
            pl.BlockSpec((tile, rows), lambda i: (i, 0)),
        ],
        out_specs=[half_spec, half_spec],
        out_shape=[half, half],
        compiler_params=VMEM,
        name="corr",
    )(place, weighted, labels_row, preds)


def put_together(place_ref, own_ref, other_ref, k):
    slot, core = place_ref[0], place_ref[1]
    own, other = own_ref[k ^ slot], other_ref[k ^ slot]
    return jnp.where(core == 0, own, other), jnp.where(core == 0, other, own)


def inverse_kernel(place_ref, count_ref, own_ref, other_ref, high_ref, low_ref, a_ref, ah_ref, al_ref, x_ref, r_ref):
    n = a_ref.shape[0]
    part = own_ref.shape[1]
    scale = 1.0 / count_ref[0]
    for k in range(own_ref.shape[0]):
        upper, lower = put_together(place_ref, own_ref, other_ref, k)
        a_ref[2 * k * part : (2 * k + 1) * part, :] = upper
        a_ref[(2 * k + 1) * part : (2 * k + 2) * part, :] = lower
    eye = jnp.where(
        lax.broadcasted_iota(jnp.int32, (n, n), 0) == lax.broadcasted_iota(jnp.int32, (n, n), 1), 1.0, 0.0
    )
    a = a_ref[...] * scale + PENALTY * eye
    a_ref[...] = a
    ah_ref[...], al_ref[...] = split(a)
    bound = jnp.max(jnp.sum(jnp.abs(a), axis=1))
    least = 0.09
    fast = bound <= FAST_NORM
    alpha = 2.0 / (bound + least)
    x_ref[...] = (2.0 * alpha) * eye - (alpha * alpha) * a
    d = (bound - least) / (bound + least)
    low = 1.0 - d * d

    def narrow(low):
        d = (1.0 - low) / (1.0 + low)
        return 1.0 - d * d

    def rough(low):
        y = x_ref[...] * (2.0 / (1.0 + low))
        yb = y.astype(jnp.bfloat16)
        r = eye - dot(ah_ref[...], yb)
        x_ref[...] = y + dot(yb, r.astype(jnp.bfloat16))
        return narrow(low)

    low = lax.while_loop(lambda low: jnp.logical_and(fast, low < 0.9), rough, low)

    def fine(carry):
        step, low, _ = carry
        y = x_ref[...] * jnp.where(low < 0.9, 2.0 / (1.0 + low), 1.0)
        yh, yl = split(y)

        @pl.when(fast)
        def _():
            r_ref[...] = eye - dot3(ah_ref[...], al_ref[...], yh, yl)

        @pl.when(jnp.logical_not(fast))
        def _():
            r_ref[...] = eye - dot(a_ref[...], y, precision=lax.Precision.HIGHEST)

        r = r_ref[...]
        rh, rl = split(r)
        x_ref[...] = y + dot3(yh, yl, rh, rl)
        return step + 1, jnp.where(low < 0.9, narrow(low), low), jnp.sum(r * r)

    lax.while_loop(
        lambda carry: jnp.logical_and(carry[0] < 40, carry[2] > 1e-5), fine, (0, low, jnp.float32(1.0))
    )
    high_ref[...], low_ref[...] = split(x_ref[...])


def make_inverse(place, count, own, other):
    cls, part, n = own.shape
    whole = pl.BlockSpec((cls, part, n), lambda: (0, 0, 0))
    smem = pl.BlockSpec(memory_space=pltpu.SMEM)
    out = jax.ShapeDtypeStruct((n, n), jnp.bfloat16)
    return pl.pallas_call(
        inverse_kernel,
        in_specs=[smem, smem, whole, whole],
        out_specs=[pl.BlockSpec((n, n), lambda: (0, 0))] * 2,
        out_shape=[out, out],
        scratch_shapes=[
            pltpu.VMEM((n, n), jnp.float32),
            pltpu.VMEM((n, n), jnp.bfloat16),
            pltpu.VMEM((n, n), jnp.bfloat16),
            pltpu.VMEM((n, n), jnp.float32),
            pltpu.VMEM((n, n), jnp.float32),
        ],
        compiler_params=VMEM,
        name="inverse",
    )(place, count, own, other)


def update_kernel(
    place_ref,
    count_ref,
    corr_own_ref,
    corr_other_ref,
    weights_ref,
    high0_ref,
    low0_ref,
    high1_ref,
    low1_ref,
    cross_own_ref,
    cross_other_ref,
    feat_ref,
    labels_ref,
    preds_ref,
    counts_ref,
    updated_ref,
    residual_ref,
    loss_ref,
    rows_ref,
    cross_high_ref,
    cross_low_ref,
):
    step = pl.program_id(0)
    tile, rows = preds_ref.shape
    slot, core, x = place_ref[0], place_ref[1], place_ref[2]
    start = slot * (tile * pl.num_programs(0)) + step * tile
    scale = 1.0 / count_ref[0]

    @pl.when(step == 0)
    def _():
        for k in range(cross_own_ref.shape[0]):
            rows16 = jnp.concatenate(put_together(place_ref, cross_own_ref, cross_other_ref, k), axis=0)
            fs = rows16.shape[0]
            cross_high_ref[k * fs : (k + 1) * fs, :], cross_low_ref[k * fs : (k + 1) * fs, :] = split(rows16)

    def sums_of(block):
        pieces = []
        for k in (2 * block, 2 * block + 1):
            own, other = corr_own_ref[k ^ x], corr_other_ref[k ^ x]
            pieces.append(jnp.where(core == 0, own, other))
            pieces.append(jnp.where(core == 0, other, own))
        return jnp.concatenate(pieces, axis=1)

    def change_of(block, sums, inv_high, inv_low):
        old = weights_ref[block].astype(jnp.float32)
        high, low = split(sums * scale - PENALTY * old)
        change = dot3(high, low, inv_high, inv_low)
        updated_ref[block] = old + change
        return change.astype(jnp.bfloat16)

    first = change_of(0, sums_of(0), high0_ref[...], low0_ref[...])
    moved = dot(first, cross_high_ref[...]) + dot(first, cross_low_ref[...])
    second = change_of(1, sums_of(1) - moved, high1_ref[...], low1_ref[...])
    residual = start_residual(start, labels_ref[...], preds_ref[...])
    residual = residual - dot(jnp.concatenate([first, second], axis=1), feat_ref[...])
    residual_ref[...] = residual
    squares = jnp.sum(residual * residual, axis=0, keepdims=True)

    @pl.when(step == 0)
    def _():
        rows_ref[...] = squares

    @pl.when(step > 0)
    def _():
        rows_ref[...] += squares

    @pl.when(step == pl.num_programs(0) - 1)
    def _():
        loss = jnp.sum(rows_ref[...] * (counts_ref[...] * scale), axis=1, keepdims=True)
        loss_ref[...] = jnp.broadcast_to(loss, loss_ref.shape)


def make_update(place, count, corr_own, corr_other, weights, inverses, cross_own, cross_other, feats, labels_row, preds, counts_row, tiles):
    width, rows = preds.shape
    total = feats.shape[0]
    n = total // 2
    cls, part, _ = cross_own.shape
    tile = width // tiles
    smem = pl.BlockSpec(memory_space=pltpu.SMEM)
    square = pl.BlockSpec((n, n), lambda i: (0, 0))
    sums = pl.BlockSpec((4, tile, total // 8), lambda i: (0, i, 0))
    cross = pl.BlockSpec((cls, part, n), lambda i: (0, 0, 0))
    row = pl.BlockSpec((1, rows), lambda i: (0, 0))
    return pl.pallas_call(
        update_kernel,
        grid=(tiles,),
        in_specs=[
            smem,
            smem,
            sums,
            sums,
            pl.BlockSpec((2, tile, n), lambda i: (0, i, 0)),
            square,
            square,
            square,
            square,
            cross,
            cross,
            pl.BlockSpec((total, rows), lambda i: (0, 0)),
            row,
            pl.BlockSpec((tile, rows), lambda i: (i, 0)),
            row,
        ],
        out_specs=[
            pl.BlockSpec((2, tile, n), lambda i: (0, i, 0)),
            pl.BlockSpec((tile, rows), lambda i: (i, 0)),
            pl.BlockSpec((1, 128), lambda i: (0, 0)),
        ],
        out_shape=[
            jax.ShapeDtypeStruct((2, width, n), jnp.float32),
            jax.ShapeDtypeStruct((width, rows), jnp.float32),
            jax.ShapeDtypeStruct((1, 128), jnp.float32),
        ],
        scratch_shapes=[
            pltpu.VMEM((1, rows), jnp.float32),
            pltpu.VMEM((n, n), jnp.bfloat16),
            pltpu.VMEM((n, n), jnp.bfloat16),
        ],
        compiler_params=VMEM,
        name="update",
    )(place, count, corr_own, corr_other, weights, *inverses, cross_own, cross_other, feats, labels_row, preds, counts_row)


def over_classes(array):
    along = gathered(array, Z)
    both = gathered(along, Y)
    return along, both.reshape(-1, *array.shape)


def per_device(
    images, image_index, labels, counts, projection, phase_shift, predictions, block_weights
):
    blocks, din, fs = projection.shape
    width = predictions.shape[1]
    rows = labels.shape[0]
    classes = width * lax.axis_size(CLS)
    core = lax.axis_index(CORE).astype(jnp.int32)
    place = jnp.stack([lax.axis_index(CLS).astype(jnp.int32), core, lax.axis_index(X).astype(jnp.int32)])

    with jax.named_scope("projection"):
        proj = jnp.pad(
            jnp.concatenate([jnp.transpose(projection, (0, 2, 1)), phase_shift[:, :, None]], axis=2),
            ((0, 0), (0, 0), (0, 127)),
        )
        _, own_proj = over_classes(lax.dynamic_index_in_dim(proj, core, 0, keepdims=False))
        other_proj = partner(own_proj, CORE, 1)

    row_weights = counts.astype(jnp.float32)
    with jax.named_scope("count"):
        count = summed(jnp.broadcast_to(jnp.sum(row_weights), (1, 128)), ROW)[0, 0:1]

    picked = images[image_index % images.shape[0]]
    counts_row = row_weights.reshape(1, rows)
    labels_row = labels.reshape(1, rows)
    preds = predictions.T
    feats, weighted, mine, theirs = make_features(place, own_proj, other_proj, picked, counts_row)

    with jax.named_scope("grams"):
        grams = summed(mine + partner(theirs, CORE, 1), X)
        with jax.named_scope("lead"):
            along, lead_own = over_classes(grams[0])
            lead_other = partner(lead_own, CORE, 1)
        rest = lax.optimization_barrier((grams[1:], along))[0]
        with jax.named_scope("rest"):
            _, rest_own = over_classes(rest)
            rest_own = jnp.moveaxis(rest_own, 1, 0)
            rest_other = partner(rest_own, CORE, 1)

    corr_mine, corr_theirs = make_corr(place, weighted, labels_row, preds, 3)
    with jax.named_scope("corr_sum"):
        halves = corr_mine + partner(corr_theirs, CORE, 1)
        send = halves.astype(jnp.bfloat16)
        total = halves[0]
        for offset in range(1, lax.axis_size(X)):
            total = total + partner(send[offset], X, offset).astype(jnp.float32)
        corr_own = gathered(total, X)
        corr_other = partner(corr_own, CORE, 1)

    inverses = [
        *make_inverse(place, count, lead_own, lead_other),
        *make_inverse(place, count, rest_own[0], rest_other[0]),
    ]
    updated, residual, loss = make_update(
        place,
        count,
        corr_own,
        corr_other,
        jnp.transpose(block_weights, (0, 2, 1)),
        inverses,
        rest_own[1],
        rest_other[1],
        feats,
        labels_row,
        preds,
        counts_row,
        3,
    )
    with jax.named_scope("loss"):
        weighted_loss = summed(summed(summed(loss, ROW), Z), Y)[0, 0] / classes
    return (jnp.transpose(updated, (0, 2, 1)), residual.T, weighted_loss)


def solution(mesh):
    cls = mesh.shape["cls"]
    row = mesh.shape["row"]
    torus = Mesh(
        mesh.devices.reshape(row // 2, 2, max(1, cls // 8), min(8, cls)), ("row_0", "row_1", "cls_0", "cls_1")
    )
    placed = (
        P(ROW, None),
        P(ROW),
        P(ROW),
        P(ROW),
        P(None, None, CLS),
        P(None, CLS),
        P(ROW, CLS),
        P(None, None, CLS),
    )
    return jax.shard_map(
        per_device,
        mesh=torus,
        in_specs=placed,
        out_specs=(P(None, None, CLS), P(ROW, CLS), P()),
        check_vma=False,
    )
```

```python
import functools

import jax
import jax.numpy as jnp
from jax import lax
from jax.experimental import pallas as pl
from jax.experimental.pallas import tpu as pltpu
from jax.sharding import Mesh
from jax.sharding import PartitionSpec as P


CLS = ("cls_0", "cls_1")
ROW = ("row_0", "row_1")
X, CORE = ROW

AMPLITUDE = 1.4142135623730951
PENALTY = 0.1
HALF_TURN_COS = (
    0.9999999997801796,
    -4.9348021370964545,
    4.0587091598532785,
    -1.3352120048696623,
    0.23493731750810104,
    -0.024396324505313864,
)
INV_TWO_PI = 0.15915494309189535
NT = (((1,), (1,)), ((), ()))
NN = (((1,), (0,)), ((), ()))
TN = (((0,), (0,)), ((), ()))
FAST_NORM = 12.0
VMEM = pltpu.CompilerParams(vmem_limit_bytes=56 << 20)


def dot(a, b, dims=NN, precision=None):
    return lax.dot_general(a, b, dims, precision=precision, preferred_element_type=jnp.float32)


def exact_dot(a, b, dims):
    return dot(a, b, dims, lax.Precision.HIGHEST)


def split(x):
    high = x.astype(jnp.bfloat16)
    low = (x - high.astype(jnp.float32)).astype(jnp.bfloat16)
    return high, low


def dot3(ah, al, bh, bl):
    return dot(ah, bh) + (dot(ah, bl) + dot(al, bh))


def scaled_cos(turns):
    f = turns - jnp.floor(turns + 0.5)
    z = f * f
    c = z * HALF_TURN_COS[5] + HALF_TURN_COS[4]
    for k in range(3, -1, -1):
        c = c * z + HALF_TURN_COS[k]
    return (2.0 * AMPLITUDE) * (c * c) - AMPLITUDE


def partner(array, axis=CORE, offset=1):
    return lax.ppermute(array, axis, [(i, i ^ offset) for i in range(lax.axis_size(axis))])


def after(array, other):
    return lax.optimization_barrier((array, other))[0]


def everyones(array, axes):
    count = lax.axis_size(axes)
    return lax.all_to_all(jnp.broadcast_to(array[None], (count, *array.shape)), axes, 0, 0, tiled=True)


def summed(array, axes):
    return jnp.sum(everyones(array, axes), axis=0)


def features_kernel(
    place_ref, own_ref, other_ref, picked_ref, counts_ref, feat_ref, weighted_ref, mine_ref, theirs_ref, proj_ref
):
    step = pl.program_id(0)
    slot, core = place_ref[0], place_ref[1]
    fs, din = own_ref.shape[1], picked_ref.shape[1]
    rows = proj_ref.shape[0]
    per = rows // fs
    inner = own_ref.shape[0] // per
    block, group = step // inner, step % inner
    for k in range(per):
        at = group * per + k
        proj_ref[k * fs : (k + 1) * fs, :] = jnp.where(
            block == core, own_ref[at].astype(jnp.float32), other_ref[at].astype(jnp.float32)
        ).astype(jnp.bfloat16)
    mixed = dot(proj_ref[:, 0:din], picked_ref[...], NT)
    phase = proj_ref[:, din : din + 1].astype(jnp.float32)
    feats = scaled_cos(mixed * INV_TWO_PI + phase * INV_TWO_PI).astype(jnp.bfloat16)
    at = pl.ds(pl.multiple_of(step * rows, rows), rows)
    feat_ref[at, :] = feats
    weighted_ref[at, :] = (feats.astype(jnp.float32) * counts_ref[...]).astype(jnp.bfloat16)

    @pl.when(step == pl.num_programs(0) - 1)
    def _():
        half = feat_ref.shape[0] // 2
        part = fs // 2
        first = pl.multiple_of(slot * fs, fs)
        lead = feat_ref[pl.ds(first, fs), :]
        later = feat_ref[pl.ds(pl.multiple_of(half + first, fs), fs), :]
        ones = jnp.ones((16, lead.shape[1]), jnp.bfloat16)
        both = dot(jnp.concatenate([lead, later, ones], axis=0), weighted_ref[...], NT)
        parts = (both[0:fs, 0:half], both[fs : 2 * fs, half:], both[0:fs, half:])
        for k, value in enumerate(parts):
            mine_ref[k] = jnp.where(core == 0, value[0:part], value[part:])
            theirs_ref[k] = jnp.where(core == 0, value[part:], value[0:part])
        row = lax.broadcasted_iota(jnp.int32, (8, half), 0)
        times = jnp.broadcast_to(counts_ref[...], ones.shape).astype(jnp.bfloat16)
        plain = dot(times, feat_ref[...], NT)[0:8]
        rounded = both[2 * fs : 2 * fs + 8]
        sums = jnp.where(row == 0, plain[:, 0:half], plain[:, half:])
        sums = jnp.where(row == 2, rounded[:, 0:half], sums)
        sums = jnp.where(row == 3, rounded[:, half:], sums)
        sums = jnp.where(row == 4, jnp.sum(counts_ref[...]), sums)
        mine_ref[3, 0:8] = sums
        theirs_ref[3, 0:8] = sums


def make_features(place, own, other, picked, counts_row):
    cls, fs, wide = own.shape
    rows, din = picked.shape
    total = 2 * cls * fs
    per = max(1, 256 // fs)
    whole = pl.BlockSpec((cls, fs, wide), lambda i: (0, 0, 0))
    part = pl.BlockSpec((4, fs // 2, total // 2), lambda i: (0, 0, 0))
    feature = pl.BlockSpec((total, rows), lambda i: (0, 0))
    return pl.pallas_call(
        features_kernel,
        grid=(2 * cls // per,),
        in_specs=[
            pl.BlockSpec(memory_space=pltpu.SMEM),
            whole,
            whole,
            pl.BlockSpec((rows, din), lambda i: (0, 0)),
            pl.BlockSpec((1, rows), lambda i: (0, 0)),
        ],
        out_specs=[feature, feature, part, part],
        out_shape=[
            jax.ShapeDtypeStruct((total, rows), jnp.bfloat16),
            jax.ShapeDtypeStruct((total, rows), jnp.bfloat16),
            jax.ShapeDtypeStruct((4, fs // 2, total // 2), jnp.float32),
            jax.ShapeDtypeStruct((4, fs // 2, total // 2), jnp.float32),
        ],
        scratch_shapes=[pltpu.VMEM((per * fs, wide), jnp.bfloat16)],
        compiler_params=VMEM,
        name="features",
    )(place, own, other, picked, counts_row)


def start_residual(start, labels, preds):
    classes = start + lax.broadcasted_iota(jnp.int32, preds.shape, 0)
    return jnp.where(labels == classes, 1.0, 0.0) - preds.astype(jnp.float32)


def corr_kernel(place_ref, weighted_ref, labels_ref, preds_ref, mine_ref, theirs_ref):
    tile = preds_ref.shape[0]
    lanes = mine_ref.shape[2]
    slot, core, x = place_ref[0], place_ref[1], place_ref[2]
    start = slot * (tile * pl.num_programs(0)) + pl.program_id(0) * tile
    residual = start_residual(start, labels_ref[...], preds_ref[...])
    sums = dot(residual.astype(jnp.bfloat16), weighted_ref[...], NT)
    for k in range(mine_ref.shape[0]):
        even = sums[:, 2 * k * lanes : (2 * k + 1) * lanes]
        odd = sums[:, (2 * k + 1) * lanes : (2 * k + 2) * lanes]
        mine_ref[k ^ x] = jnp.where(core == 0, even, odd)
        theirs_ref[k ^ x] = jnp.where(core == 0, odd, even)


def make_corr(place, weighted, labels_row, preds, tiles):
    width, rows = preds.shape
    total = weighted.shape[0]
    tile = width // tiles
    half = jax.ShapeDtypeStruct((4, width, total // 8), jnp.float32)
    half_spec = pl.BlockSpec((4, tile, total // 8), lambda i: (0, i, 0))
    return pl.pallas_call(
        corr_kernel,
        grid=(tiles,),
        in_specs=[
            pl.BlockSpec(memory_space=pltpu.SMEM),
            pl.BlockSpec((total, rows), lambda i: (0, 0)),
            pl.BlockSpec((1, rows), lambda i: (0, 0)),
            pl.BlockSpec((tile, rows), lambda i: (i, 0)),
        ],
        out_specs=[half_spec, half_spec],
        out_shape=[half, half],
        compiler_params=VMEM,
        cost_estimate=pl.CostEstimate(flops=2 * width * rows * total, transcendentals=0, bytes_accessed=8 * width * total),
        name="corr",
    )(place, weighted, labels_row, preds)


def put_together(place_ref, own_ref, other_ref, k):
    core = place_ref[1]
    own, other = own_ref[k], other_ref[k]
    return jnp.where(core == 0, own, other), jnp.where(core == 0, other, own)


def inverse_kernel(place_ref, count_ref, totals_ref, own_ref, other_ref, high_ref, low_ref, a_ref, ah_ref, al_ref, x_ref, *, block):
    n = x_ref.shape[0]
    part = own_ref.shape[1]
    scale = 1.0 / count_ref[0]
    for k in range(own_ref.shape[0]):
        upper, lower = put_together(place_ref, own_ref, other_ref, k)
        x_ref[2 * k * part : (2 * k + 1) * part, :] = upper
        x_ref[(2 * k + 1) * part : (2 * k + 2) * part, :] = lower
    row = lax.broadcasted_iota(jnp.int32, (n, n), 0)
    eye = jnp.where(row == lax.broadcasted_iota(jnp.int32, (n, n), 1), 1.0, 0.0)
    chosen = lax.broadcasted_iota(jnp.int32, totals_ref.shape, 0)
    plain = jnp.where(chosen == 0, totals_ref[block : block + 1, :] * scale, 0.0)
    rounded = jnp.where(chosen == 0, totals_ref[block + 2 : block + 3, :] * scale, 0.0)
    a = (x_ref[...] * scale + PENALTY * eye) - exact_dot(plain, rounded, TN)
    a_ref[...] = a
    ah_ref[...], al_ref[...] = split(a)
    bound = jnp.maximum(jnp.max(jnp.sum(jnp.abs(a), axis=1)), 0.1)
    least = 0.09
    fast = bound <= FAST_NORM

    def stretch(low):
        return 1.96 / (1.0 + low)

    def narrow(low):
        y = low * stretch(low)
        return y * (2.0 - y)

    low = least / bound
    alpha = stretch(low) / bound
    x_ref[...] = (2.0 * alpha) * eye - (alpha * alpha) * a
    low = narrow(low)

    def rough(low):
        y = x_ref[...] * stretch(low)
        yb = y.astype(jnp.bfloat16)
        r = eye - dot(ah_ref[...], yb)
        x_ref[...] = y + dot(yb, r.astype(jnp.bfloat16))
        return narrow(low)

    low = lax.while_loop(lambda low: jnp.logical_and(fast, low < 0.9), rough, low)

    def fine(carry):
        step, _ = carry
        x = x_ref[...]
        xh, xl = split(x)
        r = eye - dot3(ah_ref[...], al_ref[...], xh, xl)
        rb = r.astype(jnp.bfloat16)
        more = r + dot(rb, rb)
        x_ref[...] = x + dot(xh, more.astype(jnp.bfloat16))
        return step + 1, jnp.sum(r * r)

    def careful(carry):
        step, low, _ = carry
        early = low < 0.9
        y = x_ref[...] * jnp.where(early, stretch(low), 1.0)
        r = eye - exact_dot(a_ref[...], y, NN)
        x_ref[...] = y + exact_dot(y, r, NN)
        return step + 1, jnp.where(early, narrow(low), low), jnp.where(early, 1.0, jnp.sum(r * r))

    far = jnp.float32(1.0)
    lax.while_loop(
        lambda carry: jnp.logical_and(carry[0] < 20, carry[1] > 1e-2), fine, (0, jnp.where(fast, far, 0.0))
    )
    lax.while_loop(
        lambda carry: jnp.logical_and(carry[0] < 40, carry[2] > 1e-5), careful, (0, low, jnp.where(fast, 0.0, far))
    )
    x = x_ref[...]
    right = exact_dot(rounded, x, NN)
    left = exact_dot(x, plain, NT)
    weight = 1.0 / (1.0 + jnp.sum(right * plain))
    high_ref[...], low_ref[...] = split(x - exact_dot(left, right * weight, NN))


def make_inverse(place, count, totals, own, other, block):
    cls, part, n = own.shape[0], own.shape[-2], own.shape[-1]
    if own.ndim == 4:
        whole = pl.BlockSpec((cls, None, part, n), lambda i: (0, 0, 0, 0))
    else:
        whole = pl.BlockSpec((cls, part, n), lambda i: (0, 0, 0))
    smem = pl.BlockSpec(memory_space=pltpu.SMEM)
    out = jax.ShapeDtypeStruct((n, n), jnp.bfloat16)
    return pl.pallas_call(
        functools.partial(inverse_kernel, block=block),
        grid=(1,),
        in_specs=[smem, smem, pl.BlockSpec((8, n), lambda i: (0, 0)), whole, whole],
        out_specs=[pl.BlockSpec((n, n), lambda i: (0, 0))] * 2,
        out_shape=[out, out],
        scratch_shapes=[
            pltpu.VMEM((n, n), jnp.float32),
            pltpu.VMEM((n, n), jnp.bfloat16),
            pltpu.VMEM((n, n), jnp.bfloat16),
            pltpu.VMEM((n, n), jnp.float32),
        ],
        compiler_params=VMEM,
        cost_estimate=pl.CostEstimate(flops=40 * 2 * n**3, transcendentals=0, bytes_accessed=12 * n * n),
        name="inverse",
    )(place, count, totals, own, other)


def update_kernel(
    place_ref,
    count_ref,
    corr_own_ref,
    corr_other_ref,
    weights_ref,
    high0_ref,
    low0_ref,
    high1_ref,
    low1_ref,
    cross_own_ref,
    cross_other_ref,
    feat_ref,
    labels_ref,
    preds_ref,
    counts_ref,
    updated_ref,
    residual_ref,
    loss_ref,
    rows_ref,
    cross_high_ref,
    cross_low_ref,
):
    step = pl.program_id(0)
    tile, _ = preds_ref.shape
    slot, core, x = place_ref[0], place_ref[1], place_ref[2]
    start = slot * (tile * pl.num_programs(0)) + step * tile
    scale = 1.0 / count_ref[0]

    @pl.when(step == 0)
    def _():
        for k in range(cross_own_ref.shape[0]):
            rows16 = jnp.concatenate(put_together(place_ref, cross_own_ref, cross_other_ref, k), axis=0)
            fs = rows16.shape[0]
            cross_high_ref[k * fs : (k + 1) * fs, :], cross_low_ref[k * fs : (k + 1) * fs, :] = split(rows16)

    def sums_of(block):
        pieces = []
        for k in (2 * block, 2 * block + 1):
            own, other = corr_own_ref[k ^ x], corr_other_ref[k ^ x]
            pieces.append(jnp.where(core == 0, own, other))
            pieces.append(jnp.where(core == 0, other, own))
        return jnp.concatenate(pieces, axis=1)

    def change_of(block, sums, inv_high, inv_low):
        old = weights_ref[block].astype(jnp.float32)
        high, low = split(sums * scale - PENALTY * old)
        change = dot3(high, low, inv_high, inv_low)
        updated_ref[block] = old + change
        return change.astype(jnp.bfloat16)

    first = change_of(0, sums_of(0), high0_ref[...], low0_ref[...])
    moved = dot(first, cross_high_ref[...]) + dot(first, cross_low_ref[...])
    second = change_of(1, sums_of(1) - moved, high1_ref[...], low1_ref[...])
    residual = start_residual(start, labels_ref[...], preds_ref[...])
    residual = residual - dot(jnp.concatenate([first, second], axis=1), feat_ref[...])
    residual_ref[...] = residual
    squares = jnp.sum(residual * residual, axis=0, keepdims=True)

    @pl.when(step == 0)
    def _():
        rows_ref[...] = squares

    @pl.when(step > 0)
    def _():
        rows_ref[...] += squares

    @pl.when(step == pl.num_programs(0) - 1)
    def _():
        loss = jnp.sum(rows_ref[...] * (counts_ref[...] * scale), axis=1, keepdims=True)
        loss_ref[...] = jnp.broadcast_to(loss, loss_ref.shape)


def make_update(place, count, corr_own, corr_other, weights, inverses, cross_own, cross_other, feats, labels_row, preds, counts_row, tiles):
    width, rows = preds.shape
    total = feats.shape[0]
    n = total // 2
    cls, _, part, _ = cross_own.shape
    tile = width // tiles
    smem = pl.BlockSpec(memory_space=pltpu.SMEM)
    square = pl.BlockSpec((n, n), lambda i: (0, 0))
    sums = pl.BlockSpec((4, tile, total // 8), lambda i: (0, i, 0))
    cross = pl.BlockSpec((cls, None, part, n), lambda i: (0, 1, 0, 0))
    row = pl.BlockSpec((1, rows), lambda i: (0, 0))
    return pl.pallas_call(
        update_kernel,
        grid=(tiles,),
        in_specs=[
            smem,
            smem,
            sums,
            sums,
            pl.BlockSpec((2, tile, n), lambda i: (0, i, 0)),
            square,
            square,
            square,
            square,
            cross,
            cross,
            pl.BlockSpec((total, rows), lambda i: (0, 0)),
            row,
            pl.BlockSpec((tile, rows), lambda i: (i, 0)),
            row,
        ],
        out_specs=[
            pl.BlockSpec((2, tile, n), lambda i: (0, i, 0)),
            pl.BlockSpec((tile, rows), lambda i: (i, 0)),
            pl.BlockSpec((1, 128), lambda i: (0, 0)),
        ],
        out_shape=[
            jax.ShapeDtypeStruct((2, width, n), jnp.float32),
            jax.ShapeDtypeStruct((width, rows), jnp.float32),
            jax.ShapeDtypeStruct((1, 128), jnp.float32),
        ],
        scratch_shapes=[
            pltpu.VMEM((1, rows), jnp.float32),
            pltpu.VMEM((n, n), jnp.bfloat16),
            pltpu.VMEM((n, n), jnp.bfloat16),
        ],
        compiler_params=VMEM,
        name="update",
    )(place, count, corr_own, corr_other, weights, *inverses, cross_own, cross_other, feats, labels_row, preds, counts_row)


def per_device(
    images, image_index, labels, counts, projection, phase_shift, predictions, block_weights
):
    width = predictions.shape[1]
    rows = labels.shape[0]
    classes = width * lax.axis_size(CLS)
    core = lax.axis_index(CORE).astype(jnp.int32)
    place = jnp.stack([lax.axis_index(CLS).astype(jnp.int32), core, lax.axis_index(X).astype(jnp.int32)])

    proj = jnp.pad(
        jnp.concatenate([jnp.transpose(projection, (0, 2, 1)), phase_shift[:, :, None]], axis=2),
        ((0, 0), (0, 0), (0, 127)),
    )
    own_proj = everyones(lax.dynamic_index_in_dim(proj, core, 0, keepdims=False), CLS)
    other_proj = partner(own_proj)

    row_weights = counts.astype(jnp.float32)

    picked = images[image_index % images.shape[0]]
    counts_row = row_weights.reshape(1, rows)
    labels_row = labels.reshape(1, rows)
    preds = predictions.T
    feats, weighted, mine, theirs = make_features(place, own_proj, other_proj, picked, counts_row)

    chip = mine + partner(theirs)
    labels_row = after(labels_row, chip)
    grams = summed(chip, X)
    totals = grams[3, 0:8]
    count = totals[4, 0:1]
    lead_own = everyones(grams[0], CLS)
    lead_other = partner(lead_own)
    rest_own = everyones(after(grams[1:3], lead_other), CLS)
    rest_other = partner(rest_own)

    corr_mine, corr_theirs = make_corr(place, weighted, labels_row, preds, 3)
    halves = after(corr_mine + partner(corr_theirs), grams)
    send = halves.astype(jnp.bfloat16)
    others = range(1, lax.axis_size(X))
    total = halves[0] + sum(partner(send[k], X, k).astype(jnp.float32) for k in others)
    corr_own = jnp.stack([total] + [partner(total, X, k) for k in others])
    corr_other = partner(corr_own)

    lead_inverse = make_inverse(place, count, totals, lead_own, lead_other, 0)
    rest_inverse = make_inverse(place, count, totals, rest_own, rest_other, 1)
    updated, residual, loss = make_update(
        place,
        count,
        corr_own,
        corr_other,
        jnp.transpose(block_weights, (0, 2, 1)),
        [*lead_inverse, *rest_inverse],
        rest_own,
        rest_other,
        feats,
        labels_row,
        preds,
        counts_row,
        3,
    )
    weighted_loss = summed(summed(loss, ROW), CLS)[0, 0] / classes
    return (jnp.transpose(updated, (0, 2, 1)), residual.T, weighted_loss)


def solution(mesh):
    cls = mesh.shape["cls"]
    row = mesh.shape["row"]
    torus = Mesh(
        mesh.devices.reshape(row // 2, 2, max(1, cls // 8), min(8, cls)), ("row_0", "row_1", "cls_0", "cls_1")
    )
    placed = (
        P(ROW, None),
        P(ROW),
        P(ROW),
        P(ROW),
        P(None, None, CLS),
        P(None, CLS),
        P(ROW, CLS),
        P(None, None, CLS),
    )
    return jax.shard_map(
        per_device,
        mesh=torus,
        in_specs=placed,
        out_specs=(P(None, None, CLS), P(ROW, CLS), P()),
        check_vma=False,
    )
```

```python
import functools

import jax
import jax.numpy as jnp
from jax import lax
from jax.experimental import pallas as pl
from jax.experimental.pallas import tpu as pltpu
from jax.sharding import Mesh
from jax.sharding import PartitionSpec as P


CLS = ("cls_0", "cls_1")
ROW = ("row_0", "row_1")
X, CORE = ROW
Y, Z = CLS

AMPLITUDE = 1.4142135623730951
PENALTY = 0.1
HALF_TURN_COS = (
    0.9999999997801796,
    -4.9348021370964545,
    4.0587091598532785,
    -1.3352120048696623,
    0.23493731750810104,
    -0.024396324505313864,
)
INV_TWO_PI = 0.15915494309189535
NT = (((1,), (1,)), ((), ()))
NN = (((1,), (0,)), ((), ()))
FAST_NORM = 12.0
VMEM = pltpu.CompilerParams(vmem_limit_bytes=56 << 20)


def dot(a, b, dims=NN, precision=None):
    return lax.dot_general(a, b, dims, precision=precision, preferred_element_type=jnp.float32)


def exact_dot(a, b, dims):
    return dot(a, b, dims, lax.Precision.HIGHEST)


def split(x):
    high = x.astype(jnp.bfloat16)
    low = (x - high.astype(jnp.float32)).astype(jnp.bfloat16)
    return high, low


def dot3(ah, al, bh, bl):
    return dot(ah, bh) + (dot(ah, bl) + dot(al, bh))


def scaled_cos(turns):
    f = turns - jnp.floor(turns + 0.5)
    z = f * f
    c = z * HALF_TURN_COS[5] + HALF_TURN_COS[4]
    for k in range(3, -1, -1):
        c = c * z + HALF_TURN_COS[k]
    return (2.0 * AMPLITUDE) * (c * c) - AMPLITUDE


def partner(array, axis=CORE, offset=1):
    return lax.ppermute(array, axis, [(i, i ^ offset) for i in range(lax.axis_size(axis))])


def after(array, other):
    return lax.optimization_barrier((array, other))[0]


def everyones(array, axes):
    count = lax.axis_size(axes)
    return lax.all_to_all(jnp.broadcast_to(array[None], (count, *array.shape)), axes, 0, 0, tiled=True)


def summed(array, axes):
    return jnp.sum(everyones(array, axes), axis=0)


def features_kernel(
    place_ref, own_ref, other_ref, picked_ref, counts_ref, feat_ref, weighted_ref, mine_ref, theirs_ref, proj_ref
):
    step = pl.program_id(0)
    slot, core = place_ref[0], place_ref[1]
    fs, din = own_ref.shape[1], picked_ref.shape[1]
    rows = proj_ref.shape[0]
    per = rows // fs
    inner = own_ref.shape[0] // per
    block, group = step // inner, step % inner
    for k in range(per):
        at = group * per + k
        proj_ref[k * fs : (k + 1) * fs, :] = jnp.where(
            block == core, own_ref[at].astype(jnp.float32), other_ref[at].astype(jnp.float32)
        ).astype(jnp.bfloat16)
    mixed = dot(proj_ref[:, 0:din], picked_ref[...], NT)
    phase = proj_ref[:, din : din + 1].astype(jnp.float32)
    feats = scaled_cos(mixed * INV_TWO_PI + phase * INV_TWO_PI).astype(jnp.bfloat16)
    at = pl.ds(pl.multiple_of(step * rows, rows), rows)
    feat_ref[at, :] = feats
    weighted_ref[at, :] = (feats.astype(jnp.float32) * counts_ref[...]).astype(jnp.bfloat16)

    @pl.when(step == pl.num_programs(0) - 1)
    def _():
        half = feat_ref.shape[0] // 2
        part = fs // 2
        first = pl.multiple_of(slot * fs, fs)
        lead = feat_ref[pl.ds(first, fs), :]
        later = feat_ref[pl.ds(pl.multiple_of(half + first, fs), fs), :]
        ones = jnp.ones((16, lead.shape[1]), jnp.bfloat16)
        both = dot(jnp.concatenate([lead, later, ones], axis=0), weighted_ref[...], NT)
        parts = (both[0:fs, 0:half], both[fs : 2 * fs, half:], both[0:fs, half:])
        for k, value in enumerate(parts):
            mine_ref[k] = jnp.where(core == 0, value[0:part], value[part:])
            theirs_ref[k] = jnp.where(core == 0, value[part:], value[0:part])
        row = lax.broadcasted_iota(jnp.int32, (8, half), 0)
        times = jnp.broadcast_to(counts_ref[...], ones.shape).astype(jnp.bfloat16)
        plain = dot(times, feat_ref[...], NT)[0:8]
        rounded = both[2 * fs : 2 * fs + 8]
        sums = jnp.where(row == 0, plain[:, 0:half], plain[:, half:])
        sums = jnp.where(row == 2, rounded[:, 0:half], sums)
        sums = jnp.where(row == 3, rounded[:, half:], sums)
        sums = jnp.where(row == 4, jnp.sum(counts_ref[...]), sums)
        mine_ref[3, 0:8] = sums
        theirs_ref[3, 0:8] = sums


def make_features(place, own, other, picked, counts_row):
    cls, fs, wide = own.shape
    rows, din = picked.shape
    total = 2 * cls * fs
    per = max(1, 256 // fs)
    whole = pl.BlockSpec((cls, fs, wide), lambda i: (0, 0, 0))
    part = pl.BlockSpec((4, fs // 2, total // 2), lambda i: (0, 0, 0))
    feature = pl.BlockSpec((total, rows), lambda i: (0, 0))
    return pl.pallas_call(
        features_kernel,
        grid=(2 * cls // per,),
        in_specs=[
            pl.BlockSpec(memory_space=pltpu.SMEM),
            whole,
            whole,
            pl.BlockSpec((rows, din), lambda i: (0, 0)),
            pl.BlockSpec((1, rows), lambda i: (0, 0)),
        ],
        out_specs=[feature, feature, part, part],
        out_shape=[
            jax.ShapeDtypeStruct((total, rows), jnp.bfloat16),
            jax.ShapeDtypeStruct((total, rows), jnp.bfloat16),
            jax.ShapeDtypeStruct((4, fs // 2, total // 2), jnp.float32),
            jax.ShapeDtypeStruct((4, fs // 2, total // 2), jnp.float32),
        ],
        scratch_shapes=[pltpu.VMEM((per * fs, wide), jnp.bfloat16)],
        compiler_params=VMEM,
        name="features",
    )(place, own, other, picked, counts_row)


def start_residual(start, labels, preds):
    classes = start + lax.broadcasted_iota(jnp.int32, preds.shape, 0)
    return jnp.where(labels == classes, 1.0, 0.0) - preds.astype(jnp.float32)


def corr_kernel(place_ref, weighted_ref, labels_ref, preds_ref, mine_ref, theirs_ref):
    tile = preds_ref.shape[0]
    lanes = mine_ref.shape[2]
    slot, core, x = place_ref[0], place_ref[1], place_ref[2]
    start = slot * (tile * pl.num_programs(0)) + pl.program_id(0) * tile
    residual = start_residual(start, labels_ref[...], preds_ref[...])
    sums = dot(residual.astype(jnp.bfloat16), weighted_ref[...], NT)
    for k in range(mine_ref.shape[0]):
        even = sums[:, 2 * k * lanes : (2 * k + 1) * lanes]
        odd = sums[:, (2 * k + 1) * lanes : (2 * k + 2) * lanes]
        mine_ref[k ^ x] = jnp.where(core == 0, even, odd)
        theirs_ref[k ^ x] = jnp.where(core == 0, odd, even)


def make_corr(place, weighted, labels_row, preds, tiles):
    width, rows = preds.shape
    total = weighted.shape[0]
    tile = width // tiles
    half = jax.ShapeDtypeStruct((4, width, total // 8), jnp.float32)
    half_spec = pl.BlockSpec((4, tile, total // 8), lambda i: (0, i, 0))
    return pl.pallas_call(
        corr_kernel,
        grid=(tiles,),
        in_specs=[
            pl.BlockSpec(memory_space=pltpu.SMEM),
            pl.BlockSpec((total, rows), lambda i: (0, 0)),
            pl.BlockSpec((1, rows), lambda i: (0, 0)),
            pl.BlockSpec((tile, rows), lambda i: (i, 0)),
        ],
        out_specs=[half_spec, half_spec],
        out_shape=[half, half],
        compiler_params=VMEM,
        cost_estimate=pl.CostEstimate(flops=2 * width * rows * total, transcendentals=0, bytes_accessed=8 * width * total),
        name="corr",
    )(place, weighted, labels_row, preds)


def put_together(place_ref, own_ref, other_ref, k):
    core = place_ref[1]
    own, other = own_ref[k], other_ref[k]
    return jnp.where(core == 0, own, other), jnp.where(core == 0, other, own)


def inverse_kernel(place_ref, count_ref, totals_ref, own_ref, other_ref, high_ref, low_ref, a_ref, ah_ref, al_ref, x_ref, *, block):
    n = x_ref.shape[0]
    part = own_ref.shape[1]
    scale = 1.0 / count_ref[0]
    for k in range(own_ref.shape[0]):
        upper, lower = put_together(place_ref, own_ref, other_ref, k)
        x_ref[2 * k * part : (2 * k + 1) * part, :] = upper
        x_ref[(2 * k + 1) * part : (2 * k + 2) * part, :] = lower
    row = lax.broadcasted_iota(jnp.int32, (n, n), 0)
    eye = jnp.where(row == lax.broadcasted_iota(jnp.int32, (n, n), 1), 1.0, 0.0)
    plain = totals_ref[block : block + 1, :] * scale
    rounded = totals_ref[block + 2 : block + 3, :] * scale
    plain_column = jnp.sum(eye * plain, axis=1, keepdims=True)
    rounded_column = jnp.sum(eye * rounded, axis=1, keepdims=True)
    a = (x_ref[...] * scale + PENALTY * eye) - plain_column * rounded
    a_ref[...] = a
    ah_ref[...], al_ref[...] = split(a)
    bound = jnp.maximum(jnp.max(jnp.sum(jnp.abs(a), axis=1)), 0.1)
    least = 0.09
    fast = bound <= FAST_NORM

    def stretch(low):
        return 1.96 / (1.0 + low)

    def narrow(low):
        y = low * stretch(low)
        return y * (2.0 - y)

    low = least / bound
    alpha = stretch(low) / bound
    x_ref[...] = (2.0 * alpha) * eye - (alpha * alpha) * a
    low = narrow(low)

    def rough(low):
        y = x_ref[...] * stretch(low)
        yb = y.astype(jnp.bfloat16)
        r = eye - dot(ah_ref[...], yb)
        x_ref[...] = y + dot(yb, r.astype(jnp.bfloat16))
        return narrow(low)

    low = lax.while_loop(lambda low: jnp.logical_and(fast, low < 0.9), rough, low)

    def fine(carry):
        step, _ = carry
        x = x_ref[...]
        xh, xl = split(x)
        r = eye - dot3(ah_ref[...], al_ref[...], xh, xl)
        rb = r.astype(jnp.bfloat16)
        more = r + dot(rb, rb)
        x_ref[...] = x + dot(xh, more.astype(jnp.bfloat16))
        return step + 1, jnp.sum(r * r)

    def careful(carry):
        step, low, _ = carry
        early = low < 0.9
        y = x_ref[...] * jnp.where(early, stretch(low), 1.0)
        r = eye - exact_dot(a_ref[...], y, NN)
        x_ref[...] = y + exact_dot(y, r, NN)
        return step + 1, jnp.where(early, narrow(low), low), jnp.where(early, 1.0, jnp.sum(r * r))

    far = jnp.float32(1.0)
    lax.while_loop(
        lambda carry: jnp.logical_and(carry[0] < 20, carry[1] > 1e-2), fine, (0, jnp.where(fast, far, 0.0))
    )
    lax.while_loop(
        lambda carry: jnp.logical_and(carry[0] < 40, carry[2] > 1e-5), careful, (0, low, jnp.where(fast, 0.0, far))
    )
    x = x_ref[...]
    right = jnp.sum(x * rounded_column, axis=0, keepdims=True)
    left = jnp.sum(x * plain, axis=1, keepdims=True)
    weight = 1.0 / (1.0 + jnp.sum(right * plain))
    high_ref[...], low_ref[...] = split(x - left * (right * weight))


def make_inverse(place, count, totals, own, other, block):
    cls, part, n = own.shape[0], own.shape[-2], own.shape[-1]
    if own.ndim == 4:
        whole = pl.BlockSpec((cls, None, part, n), lambda i: (0, 0, 0, 0))
    else:
        whole = pl.BlockSpec((cls, part, n), lambda i: (0, 0, 0))
    smem = pl.BlockSpec(memory_space=pltpu.SMEM)
    out = jax.ShapeDtypeStruct((n, n), jnp.bfloat16)
    return pl.pallas_call(
        functools.partial(inverse_kernel, block=block),
        grid=(1,),
        in_specs=[smem, smem, pl.BlockSpec((8, n), lambda i: (0, 0)), whole, whole],
        out_specs=[pl.BlockSpec((n, n), lambda i: (0, 0))] * 2,
        out_shape=[out, out],
        scratch_shapes=[
            pltpu.VMEM((n, n), jnp.float32),
            pltpu.VMEM((n, n), jnp.bfloat16),
            pltpu.VMEM((n, n), jnp.bfloat16),
            pltpu.VMEM((n, n), jnp.float32),
        ],
        compiler_params=VMEM,
        cost_estimate=pl.CostEstimate(flops=40 * 2 * n**3, transcendentals=0, bytes_accessed=12 * n * n),
        name="inverse",
    )(place, count, totals, own, other)


def update_kernel(
    place_ref,
    count_ref,
    corr_own_ref,
    corr_other_ref,
    weights_ref,
    high0_ref,
    low0_ref,
    high1_ref,
    low1_ref,
    cross_own_ref,
    cross_other_ref,
    feat_ref,
    labels_ref,
    preds_ref,
    counts_ref,
    updated_ref,
    residual_ref,
    loss_ref,
    rows_ref,
    cross_high_ref,
    cross_low_ref,
):
    step = pl.program_id(0)
    tile, _ = preds_ref.shape
    slot, core, x = place_ref[0], place_ref[1], place_ref[2]
    start = slot * (tile * pl.num_programs(0)) + step * tile
    scale = 1.0 / count_ref[0]

    @pl.when(step == 0)
    def _():
        for k in range(cross_own_ref.shape[0]):
            rows16 = jnp.concatenate(put_together(place_ref, cross_own_ref, cross_other_ref, k), axis=0)
            fs = rows16.shape[0]
            cross_high_ref[k * fs : (k + 1) * fs, :], cross_low_ref[k * fs : (k + 1) * fs, :] = split(rows16)

    def sums_of(block):
        pieces = []
        for k in (2 * block, 2 * block + 1):
            own, other = corr_own_ref[k ^ x], corr_other_ref[k ^ x]
            pieces.append(jnp.where(core == 0, own, other))
            pieces.append(jnp.where(core == 0, other, own))
        return jnp.concatenate(pieces, axis=1)

    def change_of(block, sums, inv_high, inv_low):
        old = weights_ref[block].astype(jnp.float32)
        high, low = split(sums * scale - PENALTY * old)
        change = dot3(high, low, inv_high, inv_low)
        updated_ref[block] = old + change
        return change.astype(jnp.bfloat16)

    first = change_of(0, sums_of(0), high0_ref[...], low0_ref[...])
    moved = dot(first, cross_high_ref[...]) + dot(first, cross_low_ref[...])
    second = change_of(1, sums_of(1) - moved, high1_ref[...], low1_ref[...])
    residual = start_residual(start, labels_ref[...], preds_ref[...])
    residual = residual - dot(jnp.concatenate([first, second], axis=1), feat_ref[...])
    residual_ref[...] = residual
    squares = jnp.sum(residual * residual, axis=0, keepdims=True)

    @pl.when(step == 0)
    def _():
        rows_ref[...] = squares

    @pl.when(step > 0)
    def _():
        rows_ref[...] += squares

    @pl.when(step == pl.num_programs(0) - 1)
    def _():
        loss = jnp.sum(rows_ref[...] * (counts_ref[...] * scale), axis=1, keepdims=True)
        loss_ref[...] = jnp.broadcast_to(loss, loss_ref.shape)


def make_update(place, count, corr_own, corr_other, weights, inverses, cross_own, cross_other, feats, labels_row, preds, counts_row, tiles):
    width, rows = preds.shape
    total = feats.shape[0]
    n = total // 2
    cls, _, part, _ = cross_own.shape
    tile = width // tiles
    smem = pl.BlockSpec(memory_space=pltpu.SMEM)
    square = pl.BlockSpec((n, n), lambda i: (0, 0))
    sums = pl.BlockSpec((4, tile, total // 8), lambda i: (0, i, 0))
    cross = pl.BlockSpec((cls, None, part, n), lambda i: (0, 1, 0, 0))
    row = pl.BlockSpec((1, rows), lambda i: (0, 0))
    return pl.pallas_call(
        update_kernel,
        grid=(tiles,),
        in_specs=[
            smem,
            smem,
            sums,
            sums,
            pl.BlockSpec((2, tile, n), lambda i: (0, i, 0)),
            square,
            square,
            square,
            square,
            cross,
            cross,
            pl.BlockSpec((total, rows), lambda i: (0, 0)),
            row,
            pl.BlockSpec((tile, rows), lambda i: (i, 0)),
            row,
        ],
        out_specs=[
            pl.BlockSpec((2, tile, n), lambda i: (0, i, 0)),
            pl.BlockSpec((tile, rows), lambda i: (i, 0)),
            pl.BlockSpec((1, 128), lambda i: (0, 0)),
        ],
        out_shape=[
            jax.ShapeDtypeStruct((2, width, n), jnp.float32),
            jax.ShapeDtypeStruct((width, rows), jnp.float32),
            jax.ShapeDtypeStruct((1, 128), jnp.float32),
        ],
        scratch_shapes=[
            pltpu.VMEM((1, rows), jnp.float32),
            pltpu.VMEM((n, n), jnp.bfloat16),
            pltpu.VMEM((n, n), jnp.bfloat16),
        ],
        compiler_params=VMEM,
        name="update",
    )(place, count, corr_own, corr_other, weights, *inverses, cross_own, cross_other, feats, labels_row, preds, counts_row)


def per_device(
    images, image_index, labels, counts, projection, phase_shift, predictions, block_weights
):
    width = predictions.shape[1]
    rows = labels.shape[0]
    classes = width * lax.axis_size(CLS)
    core = lax.axis_index(CORE).astype(jnp.int32)
    place = jnp.stack([lax.axis_index(CLS).astype(jnp.int32), core, lax.axis_index(X).astype(jnp.int32)])

    proj = jnp.pad(
        jnp.concatenate([jnp.transpose(projection, (0, 2, 1)), phase_shift[:, :, None]], axis=2),
        ((0, 0), (0, 0), (0, 127)),
    )
    along = everyones(lax.dynamic_index_in_dim(proj, core, 0, keepdims=False), Z)
    own_proj = everyones(along, Y)
    own_proj = own_proj.reshape(-1, *own_proj.shape[2:])
    other_proj = partner(own_proj)

    row_weights = counts.astype(jnp.float32)

    picked = images[image_index % images.shape[0]]
    counts_row = row_weights.reshape(1, rows)
    labels_row = labels.reshape(1, rows)
    preds = predictions.T
    feats, weighted, mine, theirs = make_features(place, own_proj, other_proj, picked, counts_row)

    chip = mine + partner(theirs)
    labels_row = after(labels_row, chip)
    grams = summed(chip, X)
    totals = grams[3, 0:8]
    count = totals[4, 0:1]
    lead_own = everyones(grams[0], CLS)
    lead_other = partner(lead_own)
    rest_own = everyones(after(grams[1:3], lead_other), CLS)
    rest_other = partner(rest_own)

    corr_mine, corr_theirs = make_corr(place, weighted, labels_row, preds, 3)
    halves = after(corr_mine + partner(corr_theirs), grams)
    others = range(1, lax.axis_size(X))
    total = halves[0] + sum(partner(halves[k], X, k) for k in others)
    corr_own = jnp.stack([total] + [partner(total, X, k) for k in others])
    corr_other = partner(corr_own)

    lead_inverse = make_inverse(place, count, totals, lead_own, lead_other, 0)
    rest_inverse = make_inverse(place, count, totals, rest_own, rest_other, 1)
    updated, residual, loss = make_update(
        place,
        count,
        corr_own,
        corr_other,
        jnp.transpose(block_weights, (0, 2, 1)),
        [*lead_inverse, *rest_inverse],
        rest_own,
        rest_other,
        feats,
        labels_row,
        preds,
        counts_row,
        3,
    )
    weighted_loss = summed(summed(summed(loss, ROW), Z), Y)[0, 0] / classes
    return (jnp.transpose(updated, (0, 2, 1)), residual.T, weighted_loss)


def solution(mesh):
    cls = mesh.shape["cls"]
    row = mesh.shape["row"]
    torus = Mesh(
        mesh.devices.reshape(row // 2, 2, max(1, cls // 8), min(8, cls)), ("row_0", "row_1", "cls_0", "cls_1")
    )
    placed = (
        P(ROW, None),
        P(ROW),
        P(ROW),
        P(ROW),
        P(None, None, CLS),
        P(None, CLS),
        P(ROW, CLS),
        P(None, None, CLS),
    )
    return jax.shard_map(
        per_device,
        mesh=torus,
        in_specs=placed,
        out_specs=(P(None, None, CLS), P(ROW, CLS), P()),
        check_vma=False,
    )
```

```python
import functools

import jax
import jax.numpy as jnp
from jax import lax
from jax.experimental import pallas as pl
from jax.experimental.pallas import tpu as pltpu
from jax.sharding import Mesh
from jax.sharding import PartitionSpec as P


CLS = ("cls_0", "cls_1")
ROW = ("row_0", "row_1")
X, CORE = ROW

AMPLITUDE = 1.4142135623730951
PENALTY = 0.1
HALF_TURN_COS = (
    0.9999999997801796,
    -4.9348021370964545,
    4.0587091598532785,
    -1.3352120048696623,
    0.23493731750810104,
    -0.024396324505313864,
)
INV_TWO_PI = 0.15915494309189535
NT = (((1,), (1,)), ((), ()))
NN = (((1,), (0,)), ((), ()))
FAST_NORM = 12.0
VMEM = pltpu.CompilerParams(vmem_limit_bytes=56 << 20)


def dot(a, b, dims=NN, precision=None):
    return lax.dot_general(a, b, dims, precision=precision, preferred_element_type=jnp.float32)


def exact_dot(a, b, dims):
    return dot(a, b, dims, lax.Precision.HIGHEST)


def split(x):
    high = x.astype(jnp.bfloat16)
    low = (x - high.astype(jnp.float32)).astype(jnp.bfloat16)
    return high, low


def dot3(ah, al, bh, bl):
    return dot(ah, bh) + (dot(ah, bl) + dot(al, bh))


def scaled_cos(turns):
    f = turns - jnp.floor(turns + 0.5)
    z = f * f
    c = z * HALF_TURN_COS[5] + HALF_TURN_COS[4]
    for k in range(3, -1, -1):
        c = c * z + HALF_TURN_COS[k]
    return (2.0 * AMPLITUDE) * (c * c) - AMPLITUDE


def partner(array, axis=CORE, offset=1):
    return lax.ppermute(array, axis, [(i, i ^ offset) for i in range(lax.axis_size(axis))])


def exchanged(array, axis):
    return [array] + [partner(array, axis, k) for k in range(1, lax.axis_size(axis))]


def after(array, other):
    return lax.optimization_barrier((array, other))[0]


def everyones(array, axes):
    count = lax.axis_size(axes)
    return lax.all_to_all(jnp.broadcast_to(array[None], (count, *array.shape)), axes, 0, 0, tiled=True)


def summed(array, axes):
    return jnp.sum(everyones(array, axes), axis=0)


def features_kernel(
    place_ref, own_ref, other_ref, picked_ref, counts_ref, feat_ref, weighted_ref, mine_ref, theirs_ref, proj_ref
):
    step = pl.program_id(0)
    slot, core, x = place_ref[0], place_ref[1], place_ref[2]
    fs, lanes = own_ref.shape[2], own_ref.shape[3]
    din = picked_ref.shape[1]
    rows = proj_ref.shape[0]
    per = rows // fs
    inner = own_ref.shape[1] // per
    block, group = step // inner, step % inner
    for k in range(per):
        device = group * per + k
        for q in range(5):
            at = q ^ x if q < 4 else q
            proj_ref[k * fs : (k + 1) * fs, q * lanes : (q + 1) * lanes] = jnp.where(
                block == core, own_ref[at, device].astype(jnp.float32), other_ref[at, device].astype(jnp.float32)
            ).astype(jnp.bfloat16)
    mixed = dot(proj_ref[:, 0:din], picked_ref[...], NT)
    phase = proj_ref[:, din : din + 1].astype(jnp.float32)
    feats = scaled_cos(mixed * INV_TWO_PI + phase * INV_TWO_PI).astype(jnp.bfloat16)
    at = pl.ds(pl.multiple_of(step * rows, rows), rows)
    feat_ref[at, :] = feats
    weighted_ref[at, :] = (feats.astype(jnp.float32) * counts_ref[...]).astype(jnp.bfloat16)

    @pl.when(step == pl.num_programs(0) - 1)
    def _():
        half = feat_ref.shape[0] // 2
        part = fs // 2
        first = pl.multiple_of(slot * fs, fs)
        lead = feat_ref[pl.ds(first, fs), :]
        later = feat_ref[pl.ds(pl.multiple_of(half + first, fs), fs), :]
        ones = jnp.ones((16, lead.shape[1]), jnp.bfloat16)
        both = dot(jnp.concatenate([lead, later, ones], axis=0), weighted_ref[...], NT)
        parts = (both[0:fs, 0:half], both[fs : 2 * fs, half:], both[0:fs, half:])
        wide = half // 4
        for k, value in enumerate(parts):
            upper = jnp.where(core == 0, value[0:part], value[part:])
            lower = jnp.where(core == 0, value[part:], value[0:part])
            for q in range(4):
                mine_ref[q, k] = upper[:, q * wide : (q + 1) * wide]
                theirs_ref[q, k] = lower[:, q * wide : (q + 1) * wide]
        row = lax.broadcasted_iota(jnp.int32, (8, half), 0)
        times = jnp.broadcast_to(counts_ref[...], ones.shape).astype(jnp.bfloat16)
        plain = dot(times, feat_ref[...], NT)[0:8]
        rounded = both[2 * fs : 2 * fs + 8]
        sums = jnp.where(row == 0, plain[:, 0:half], plain[:, half:])
        sums = jnp.where(row == 2, rounded[:, 0:half], sums)
        sums = jnp.where(row == 3, rounded[:, half:], sums)
        sums = jnp.where(row == 4, jnp.sum(counts_ref[...]), sums)
        for q in range(4):
            mine_ref[q, 3, 0:8] = sums[:, q * wide : (q + 1) * wide]
            theirs_ref[q, 3, 0:8] = sums[:, q * wide : (q + 1) * wide]


def make_features(place, own, other, picked, counts_row):
    _, cls, fs, lanes = own.shape
    rows, din = picked.shape
    total = 2 * cls * fs
    per = max(1, 256 // fs)
    whole = pl.BlockSpec(own.shape, lambda i: (0, 0, 0, 0))
    grams = (4, 4, fs // 2, total // 8)
    part = pl.BlockSpec(grams, lambda i: (0, 0, 0, 0))
    feature = pl.BlockSpec((total, rows), lambda i: (0, 0))
    return pl.pallas_call(
        features_kernel,
        grid=(2 * cls // per,),
        in_specs=[
            pl.BlockSpec(memory_space=pltpu.SMEM),
            whole,
            whole,
            pl.BlockSpec((rows, din), lambda i: (0, 0)),
            pl.BlockSpec((1, rows), lambda i: (0, 0)),
        ],
        out_specs=[feature, feature, part, part],
        out_shape=[
            jax.ShapeDtypeStruct((total, rows), jnp.bfloat16),
            jax.ShapeDtypeStruct((total, rows), jnp.bfloat16),
            jax.ShapeDtypeStruct(grams, jnp.float32),
            jax.ShapeDtypeStruct(grams, jnp.float32),
        ],
        scratch_shapes=[pltpu.VMEM((per * fs, 5 * lanes), jnp.bfloat16)],
        compiler_params=VMEM,
        name="features",
    )(place, own, other, picked, counts_row)


def start_residual(start, labels, preds):
    classes = start + lax.broadcasted_iota(jnp.int32, preds.shape, 0)
    return jnp.where(labels == classes, 1.0, 0.0) - preds.astype(jnp.float32)


def corr_kernel(place_ref, weighted_ref, labels_ref, preds_ref, mine_ref, theirs_ref):
    tile = preds_ref.shape[0]
    lanes = mine_ref.shape[2]
    slot, core, x = place_ref[0], place_ref[1], place_ref[2]
    start = slot * (tile * pl.num_programs(0)) + pl.program_id(0) * tile
    residual = start_residual(start, labels_ref[...], preds_ref[...])
    sums = dot(residual.astype(jnp.bfloat16), weighted_ref[...], NT)
    for k in range(mine_ref.shape[0]):
        even = sums[:, 2 * k * lanes : (2 * k + 1) * lanes]
        odd = sums[:, (2 * k + 1) * lanes : (2 * k + 2) * lanes]
        mine_ref[k ^ x] = jnp.where(core == 0, even, odd)
        theirs_ref[k ^ x] = jnp.where(core == 0, odd, even)


def make_corr(place, weighted, labels_row, preds, tiles):
    width, rows = preds.shape
    total = weighted.shape[0]
    tile = width // tiles
    half = jax.ShapeDtypeStruct((4, width, total // 8), jnp.float32)
    half_spec = pl.BlockSpec((4, tile, total // 8), lambda i: (0, i, 0))
    return pl.pallas_call(
        corr_kernel,
        grid=(tiles,),
        in_specs=[
            pl.BlockSpec(memory_space=pltpu.SMEM),
            pl.BlockSpec((total, rows), lambda i: (0, 0)),
            pl.BlockSpec((1, rows), lambda i: (0, 0)),
            pl.BlockSpec((tile, rows), lambda i: (i, 0)),
        ],
        out_specs=[half_spec, half_spec],
        out_shape=[half, half],
        compiler_params=VMEM,
        cost_estimate=pl.CostEstimate(flops=2 * width * rows * total, transcendentals=0, bytes_accessed=8 * width * total),
        name="corr",
    )(place, weighted, labels_row, preds)


def put_together(place_ref, own_ref, other_ref, whole_ref):
    core, x = place_ref[1], place_ref[2]
    part, wide = own_ref.shape[-2:]
    for q in range(4):
        for k in range(whole_ref.shape[0] // (2 * part)):
            own, other = own_ref[q ^ x, k], other_ref[q ^ x, k]
            columns = slice(q * wide, (q + 1) * wide)
            whole_ref[2 * k * part : (2 * k + 1) * part, columns] = jnp.where(core == 0, own, other)
            whole_ref[(2 * k + 1) * part : (2 * k + 2) * part, columns] = jnp.where(core == 0, other, own)


def inverse_kernel(place_ref, count_ref, totals_ref, own_ref, other_ref, high_ref, low_ref, a_ref, ah_ref, al_ref, x_ref, *, block):
    n = x_ref.shape[0]
    scale = 1.0 / count_ref[0]
    put_together(place_ref, own_ref, other_ref, x_ref)
    x = place_ref[2]
    totals = jnp.concatenate([totals_ref[q ^ x] for q in range(4)], axis=1)
    row = lax.broadcasted_iota(jnp.int32, (n, n), 0)
    eye = jnp.where(row == lax.broadcasted_iota(jnp.int32, (n, n), 1), 1.0, 0.0)
    plain = totals[block : block + 1, :] * scale
    rounded = totals[block + 2 : block + 3, :] * scale
    plain_column = jnp.sum(eye * plain, axis=1, keepdims=True)
    rounded_column = jnp.sum(eye * rounded, axis=1, keepdims=True)
    a = (x_ref[...] * scale + PENALTY * eye) - plain_column * rounded
    a_ref[...] = a
    ah_ref[...], al_ref[...] = split(a)
    bound = jnp.maximum(jnp.max(jnp.sum(jnp.abs(a), axis=1)), 0.1)
    least = 0.09
    fast = bound <= FAST_NORM

    def stretch(low):
        return 1.96 / (1.0 + low)

    def narrow(low):
        y = low * stretch(low)
        return y * (2.0 - y)

    low = least / bound
    alpha = stretch(low) / bound
    x_ref[...] = (2.0 * alpha) * eye - (alpha * alpha) * a
    low = narrow(low)

    def rough(low):
        y = x_ref[...] * stretch(low)
        yb = y.astype(jnp.bfloat16)
        r = eye - dot(ah_ref[...], yb)
        x_ref[...] = y + dot(yb, r.astype(jnp.bfloat16))
        return narrow(low)

    low = lax.while_loop(lambda low: jnp.logical_and(fast, low < 0.97), rough, low)

    def fine(carry):
        step, _ = carry
        x = x_ref[...]
        xh, xl = split(x)
        r = eye - dot3(ah_ref[...], al_ref[...], xh, xl)
        rb = r.astype(jnp.bfloat16)
        more = r + dot(rb, rb)
        x_ref[...] = x + dot(xh, more.astype(jnp.bfloat16))
        return step + 1, jnp.sum(r * r)

    def careful(carry):
        step, low, _ = carry
        early = low < 0.9
        y = x_ref[...] * jnp.where(early, stretch(low), 1.0)
        r = eye - exact_dot(a_ref[...], y, NN)
        x_ref[...] = y + exact_dot(y, r, NN)
        return step + 1, jnp.where(early, narrow(low), low), jnp.where(early, 1.0, jnp.sum(r * r))

    far = jnp.float32(1.0)
    lax.while_loop(
        lambda carry: jnp.logical_and(carry[0] < 20, carry[1] > 3e-2), fine, (0, jnp.where(fast, far, 0.0))
    )
    lax.while_loop(
        lambda carry: jnp.logical_and(carry[0] < 40, carry[2] > 1e-5), careful, (0, low, jnp.where(fast, 0.0, far))
    )
    x = x_ref[...]
    right = jnp.sum(x * rounded_column, axis=0, keepdims=True)
    left = jnp.sum(x * plain, axis=1, keepdims=True)
    weight = 1.0 / (1.0 + jnp.sum(right * plain))
    high_ref[...], low_ref[...] = split(x - left * (right * weight))


def make_inverse(place, count, totals, own, other, block):
    part, wide = own.shape[-2:]
    n = 4 * wide
    if own.ndim == 5:
        whole = pl.BlockSpec((4, own.shape[1], None, part, wide), lambda i: (0, 0, 0, 0, 0))
    else:
        whole = pl.BlockSpec(own.shape, lambda i: (0, 0, 0, 0))
    smem = pl.BlockSpec(memory_space=pltpu.SMEM)
    out = jax.ShapeDtypeStruct((n, n), jnp.bfloat16)
    return pl.pallas_call(
        functools.partial(inverse_kernel, block=block),
        grid=(1,),
        in_specs=[smem, smem, pl.BlockSpec((4, 8, wide), lambda i: (0, 0, 0)), whole, whole],
        out_specs=[pl.BlockSpec((n, n), lambda i: (0, 0))] * 2,
        out_shape=[out, out],
        scratch_shapes=[
            pltpu.VMEM((n, n), jnp.float32),
            pltpu.VMEM((n, n), jnp.bfloat16),
            pltpu.VMEM((n, n), jnp.bfloat16),
            pltpu.VMEM((n, n), jnp.float32),
        ],
        compiler_params=VMEM,
        cost_estimate=pl.CostEstimate(flops=40 * 2 * n**3, transcendentals=0, bytes_accessed=12 * n * n),
        name="inverse",
    )(place, count, totals, own, other)


def update_kernel(
    place_ref,
    count_ref,
    corr_own_ref,
    corr_other_ref,
    weights_ref,
    high0_ref,
    low0_ref,
    high1_ref,
    low1_ref,
    cross_own_ref,
    cross_other_ref,
    feat_ref,
    labels_ref,
    preds_ref,
    counts_ref,
    updated_ref,
    residual_ref,
    loss_ref,
    rows_ref,
    cross_ref,
    cross_high_ref,
    cross_mid_ref,
    cross_low_ref,
):
    step = pl.program_id(0)
    tile, _ = preds_ref.shape
    slot, core, x = place_ref[0], place_ref[1], place_ref[2]
    start = slot * (tile * pl.num_programs(0)) + step * tile
    scale = 1.0 / count_ref[0]

    @pl.when(step == 0)
    def _():
        put_together(place_ref, cross_own_ref, cross_other_ref, cross_ref)
        cross = cross_ref[...]
        high, rest = split(cross)
        cross_high_ref[...] = high
        cross_mid_ref[...] = rest
        cross_low_ref[...] = ((cross - high.astype(jnp.float32)) - rest.astype(jnp.float32)).astype(jnp.bfloat16)

    def sums_of(block):
        pieces = []
        for k in (2 * block, 2 * block + 1):
            own, other = corr_own_ref[k ^ x], corr_other_ref[k ^ x]
            pieces.append(jnp.where(core == 0, own, other))
            pieces.append(jnp.where(core == 0, other, own))
        return jnp.concatenate(pieces, axis=1)

    def change_of(block, sums, inv_high, inv_low):
        old = weights_ref[block].astype(jnp.float32)
        high, low = split(sums * scale - PENALTY * old)
        change = dot3(high, low, inv_high, inv_low)
        updated_ref[block] = old + change
        return change.astype(jnp.bfloat16)

    first = change_of(0, sums_of(0), high0_ref[...], low0_ref[...])
    moved = dot(first, cross_high_ref[...]) + (dot(first, cross_mid_ref[...]) + dot(first, cross_low_ref[...]))
    second = change_of(1, sums_of(1) - moved, high1_ref[...], low1_ref[...])
    residual = start_residual(start, labels_ref[...], preds_ref[...])
    residual = residual - dot(jnp.concatenate([first, second], axis=1), feat_ref[...])
    residual_ref[...] = residual
    squares = jnp.sum(residual * residual, axis=0, keepdims=True)

    @pl.when(step == 0)
    def _():
        rows_ref[...] = squares

    @pl.when(step > 0)
    def _():
        rows_ref[...] += squares

    @pl.when(step == pl.num_programs(0) - 1)
    def _():
        loss = jnp.sum(rows_ref[...] * (counts_ref[...] * scale), axis=1, keepdims=True)
        loss_ref[...] = jnp.broadcast_to(loss, loss_ref.shape)


def make_update(place, count, corr_own, corr_other, weights, inverses, cross_own, cross_other, feats, labels_row, preds, counts_row, tiles):
    width, rows = preds.shape
    total = feats.shape[0]
    n = total // 2
    _, cls, _, part, wide = cross_own.shape
    tile = width // tiles
    smem = pl.BlockSpec(memory_space=pltpu.SMEM)
    square = pl.BlockSpec((n, n), lambda i: (0, 0))
    sums = pl.BlockSpec((4, tile, total // 8), lambda i: (0, i, 0))
    cross = pl.BlockSpec((4, cls, None, part, wide), lambda i: (0, 0, 1, 0, 0))
    row = pl.BlockSpec((1, rows), lambda i: (0, 0))
    return pl.pallas_call(
        update_kernel,
        grid=(tiles,),
        in_specs=[
            smem,
            smem,
            sums,
            sums,
            pl.BlockSpec((2, tile, n), lambda i: (0, i, 0)),
            square,
            square,
            square,
            square,
            cross,
            cross,
            pl.BlockSpec((total, rows), lambda i: (0, 0)),
            row,
            pl.BlockSpec((tile, rows), lambda i: (i, 0)),
            row,
        ],
        out_specs=[
            pl.BlockSpec((2, tile, n), lambda i: (0, i, 0)),
            pl.BlockSpec((tile, rows), lambda i: (i, 0)),
            pl.BlockSpec((1, 128), lambda i: (0, 0)),
        ],
        out_shape=[
            jax.ShapeDtypeStruct((2, width, n), jnp.float32),
            jax.ShapeDtypeStruct((width, rows), jnp.float32),
            jax.ShapeDtypeStruct((1, 128), jnp.float32),
        ],
        scratch_shapes=[
            pltpu.VMEM((1, rows), jnp.float32),
            pltpu.VMEM((n, n), jnp.float32),
            pltpu.VMEM((n, n), jnp.bfloat16),
            pltpu.VMEM((n, n), jnp.bfloat16),
            pltpu.VMEM((n, n), jnp.bfloat16),
        ],
        compiler_params=VMEM,
        name="update",
    )(place, count, corr_own, corr_other, weights, *inverses, cross_own, cross_other, feats, labels_row, preds, counts_row)


def per_device(
    images, image_index, labels, counts, projection, phase_shift, predictions, block_weights
):
    _, din, fs = projection.shape
    width = predictions.shape[1]
    rows = labels.shape[0]
    classes = width * lax.axis_size(CLS)
    core = lax.axis_index(CORE).astype(jnp.int32)
    place = jnp.stack([lax.axis_index(CLS).astype(jnp.int32), core, lax.axis_index(X).astype(jnp.int32)])

    x = lax.axis_index(X)
    quarter = lax.dynamic_slice(jnp.transpose(projection, (0, 2, 1)), (core, 0, x * (din // 4)), (1, fs, din // 4))
    phase = lax.dynamic_slice(phase_shift, (core, 0), (1, fs))
    shard = jnp.concatenate([quarter, jnp.broadcast_to(phase[:, :, None], quarter.shape)])
    everything = everyones(shard, CLS)
    own_proj = jnp.stack(exchanged(everything[:, 0], X) + [everything[:, 1]])
    other_proj = partner(own_proj)

    row_weights = counts.astype(jnp.float32)

    picked = images[image_index % images.shape[0]]
    counts_row = row_weights.reshape(1, rows)
    labels_row = labels.reshape(1, rows)
    preds = predictions.T
    feats, weighted, mine, theirs = make_features(place, own_proj, other_proj, picked, counts_row)

    chip = mine + partner(theirs)
    labels_row = after(labels_row, chip)
    grams = jnp.sum(lax.all_to_all(chip, X, 0, 0, tiled=True), axis=0)
    count = grams[3, 4, 0:1]
    everything = everyones(grams[0:3], CLS)
    lead_own = jnp.stack(exchanged(jnp.concatenate([everything[:, 0], grams[3:4, 0:8]]), X))
    totals = lead_own[:, -1]
    lead_other = partner(lead_own)
    rest_own = jnp.stack(exchanged(everything[:, 1:3], X))
    rest_other = partner(rest_own)

    corr_mine, corr_theirs = make_corr(place, weighted, labels_row, preds, 3)
    halves = after(corr_mine + partner(corr_theirs), grams)
    others = range(1, lax.axis_size(X))
    total = halves[0] + sum(partner(halves[k], X, k) for k in others)
    corr_own = jnp.stack(exchanged(total, X))
    corr_other = partner(corr_own)

    lead_inverse = make_inverse(place, count, totals, lead_own, lead_other, 0)
    rest_inverse = make_inverse(place, count, totals, rest_own, rest_other, 1)
    updated, residual, loss = make_update(
        place,
        count,
        corr_own,
        corr_other,
        jnp.transpose(block_weights, (0, 2, 1)),
        [*lead_inverse, *rest_inverse],
        rest_own,
        rest_other,
        feats,
        labels_row,
        preds,
        counts_row,
        3,
    )
    weighted_loss = summed(summed(loss, ROW), CLS)[0, 0] / classes
    return (jnp.transpose(updated, (0, 2, 1)), residual.T, weighted_loss)


def solution(mesh):
    cls = mesh.shape["cls"]
    row = mesh.shape["row"]
    torus = Mesh(
        mesh.devices.reshape(row // 2, 2, max(1, cls // 8), min(8, cls)), ("row_0", "row_1", "cls_0", "cls_1")
    )
    placed = (
        P(ROW, None),
        P(ROW),
        P(ROW),
        P(ROW),
        P(None, None, CLS),
        P(None, CLS),
        P(ROW, CLS),
        P(None, None, CLS),
    )
    return jax.shard_map(
        per_device,
        mesh=torus,
        in_specs=placed,
        out_specs=(P(None, None, CLS), P(ROW, CLS), P()),
        check_vma=False,
    )
```
